32 devices in a mesh: parts: 2 (over y), wide: 4 (over x, core), narrow: 4 (over z).
Axes of the slice: x: 2, y: 2, z: 4, core: 2. Of those that a mesh axis runs over, the one named last changes fastest.
Arguments:
- hist_events: bfloat16 [8, 2048, 512], P(('parts', 'wide'), 'narrow'), parts along dimension 0, may hold values from -6 to 6
- query_events: bfloat16 [8, 1024, 512], P(('parts', 'wide'), 'narrow'), parts along dimension 0, may hold values from -6 to 6
- hist_lengths: int32 [8], P(('parts', 'wide')), parts along dimension 0, may hold values from 512 to 2048
- time_buckets: int32 [8, 2048], P(('parts', 'wide'), 'narrow'), parts along dimension 0, may hold values from 0 to 127
- w_key: bfloat16 [512, 1024], replicated, may hold values from -0.25 to 0.25
- w_query: bfloat16 [512, 1024], replicated, may hold values from -0.25 to 0.25
- bias_table: bfloat16 [128, 8], replicated, may hold values from -3 to 3
- out_gain: float32 [512], replicated, may hold values from 0.1 to 1.9
- w_out: bfloat16 [512, 512], replicated, may hold values from -0.25 to 0.25
Outputs:
- layer_out: bfloat16 [8, 1024, 512], P(('parts', 'wide'), 'narrow'), parts along dimension 0
The draws below stay inside these ranges and needn't reach their ends.
There are 2 independent parts, one for each index of `parts`. The reference program is written for one: setup_inputs(seed, part) draws one part's arguments, and reference() takes and returns one part's arrays. A program takes and returns all parts, laid end to end along the dimension named above; an argument that names none is the same for every part. Nothing has to cross between parts.
All inputs are finite; a program needn't handle non-finite values.
Results may differ from the reference program's by a relative error of at most 0.0048.
Values may be sent and summed in bfloat16 or wider, within the bound.
A program may use at most 128 MiB of HBM per device.

```python
import math
import jax
import jax.numpy as jnp
from jax import lax

D = 512
HEADS = 8
BUCKETS = 128
USERS = 4
HIST = 2048
QUERIES = 1024


def place_ends(values, rng, low, largest):
    longest = values.shape.index(max(values.shape))
    spots = []
    for shift in (0, 1):
        where = [jax.random.randint(jax.random.fold_in(rng, axis), (), 0, length) for axis, length in enumerate(values.shape)]
        where[longest] = (where[longest] + shift) % values.shape[longest]
        spots.append(tuple(where))
    return values.at[spots[0]].set(low).at[spots[1]].set(largest)


def block_scale(own_key, extent, split, low, high):
    level, own = 1.0, jax.random.fold_in(own_key, 6)
    for axis_at, parts in split:
        steps = jnp.exp(jax.random.uniform(jax.random.fold_in(own, axis_at), (parts,), jnp.float32, low / len(split), high / len(split)))
        level = level * jnp.repeat(steps, extent[axis_at] // parts).reshape([-1 if axis == axis_at else 1 for axis in range(len(extent))])
    return level


def normal_values(own_key, shape, width, reach, shards=(), kind=jnp.bfloat16):
    gain = block_scale(own_key, shape, shards, -0.22, 0.18) if shards else 1.0
    drawn = jax.random.normal(own_key, shape, jnp.float32) * width * gain
    return jnp.minimum(jnp.maximum(drawn, -reach), reach).astype(kind)


def setup_inputs(seed: int = 0, part: int = 0) -> dict:
    key_list = jax.random.split(jax.random.key(seed), 10)
    part_keys = jax.random.split(jax.random.fold_in(key_list[9], part), 10)
    return {
        "hist_events": normal_values(part_keys[0], (USERS, HIST, D), 1.0, 6.0, ((0, 4), (1, 4))),
        "query_events": normal_values(part_keys[1], (USERS, QUERIES, D), 1.0, 6.0, ((0, 4), (1, 4))),
        "hist_lengths": place_ends(jax.random.randint(part_keys[2], (USERS,), HIST // 4, HIST + 1), jax.random.fold_in(part_keys[2], 1), HIST // 4, HIST).astype(jnp.int32),
        "time_buckets": place_ends(jax.random.randint(part_keys[3], (USERS, HIST), 0, BUCKETS), jax.random.fold_in(part_keys[3], 1), 0, BUCKETS - 1).astype(jnp.int32),
        "w_key": normal_values(key_list[4], (D, 2 * D), D ** -0.5, 0.25),
        "w_query": normal_values(key_list[5], (D, 2 * D), D ** -0.5, 0.25),
        "bias_table": normal_values(key_list[6], (BUCKETS, HEADS), 1.0, 3.0),
        "out_gain": jnp.clip(1.0 + 0.18 * jax.random.normal(key_list[7], (D,), jnp.float32), 0.1, 1.9),
        "w_out": normal_values(key_list[8], (D, D), D ** -0.5, 0.25),
    }


def user_output(history, queries_in, length, buckets, w_key, w_query, bias_table, out_gain, w_out):
    head_size = D // HEADS
    score_scale = 1.0 / math.sqrt(head_size)
    key_value = jnp.dot(history, w_key, preferred_element_type=jnp.float32)
    key_states = lax.optimization_barrier(jax.nn.silu(key_value[:, :D]).astype(jnp.bfloat16))
    value_states = lax.optimization_barrier(key_value[:, D:].astype(jnp.bfloat16))
    query_gate = jnp.dot(queries_in, w_query, preferred_element_type=jnp.float32)
    query_states = lax.optimization_barrier(jax.nn.silu(query_gate[:, :D]).astype(jnp.bfloat16))
    gate_states = jax.nn.silu(query_gate[:, D:])
    bias_keys = bias_table[buckets].astype(jnp.float32)
    block_rows = 128 if HIST % 128 == 0 else HIST
    blocks = HIST // block_rows
    query_heads = query_states.astype(jnp.float32).reshape(QUERIES, HEADS, head_size)
    key_blocks = key_states.astype(jnp.float32).reshape(blocks, block_rows, HEADS, head_size)
    value_blocks = value_states.astype(jnp.float32).reshape(blocks, block_rows, HEADS, head_size)
    bias_blocks = bias_keys.reshape(blocks, block_rows, HEADS)

    def absorb_block(running, item):
        key_block, value_block, bias_block, block_index = item
        scores = jnp.einsum('qhd,khd->hqk', query_heads, key_block, precision=lax.Precision.HIGHEST)
        scores = scores * score_scale + bias_block.T[:, None, :]
        position = block_index * block_rows + jnp.arange(block_rows, dtype=jnp.int32)
        live = (position < length).astype(jnp.float32)
        weights = lax.optimization_barrier((jax.nn.silu(scores) * live[None, None, :]).astype(jnp.bfloat16))
        contrib = jnp.einsum('hqk,khd->qhd', weights.astype(jnp.float32), value_block, precision=lax.Precision.HIGHEST)
        return (running + contrib, None)
    running, _ = lax.scan(absorb_block, jnp.zeros((QUERIES, HEADS, head_size), jnp.float32), (key_blocks, value_blocks, bias_blocks, jnp.arange(blocks, dtype=jnp.int32)))
    attended = running.reshape(QUERIES, D)
    center = lax.optimization_barrier(jnp.mean(attended, axis=-1, keepdims=True))
    spread = lax.optimization_barrier(jnp.mean(jnp.square(attended - center), axis=-1, keepdims=True))
    normed = (attended - center) * lax.rsqrt(spread + 1e-05)
    mixed = (normed * out_gain * gate_states).astype(jnp.bfloat16)
    return (queries_in.astype(jnp.float32) + jnp.dot(mixed, w_out, preferred_element_type=jnp.float32)).astype(jnp.bfloat16)

def reference(hist_events, query_events, hist_lengths, time_buckets, w_key, w_query, bias_table, out_gain, w_out):

    def one_user(item):
        history, queries_in, length, buckets = item
        return user_output(history, queries_in, length, buckets, w_key, w_query, bias_table, out_gain, w_out)
    return lax.map(one_user, (hist_events, query_events, hist_lengths, time_buckets))
```

```python
import functools
import math

import jax
import jax.numpy as jnp
from jax import lax
from jax.experimental import pallas as pl
from jax.experimental.pallas import tpu as pltpu
from jax.sharding import PartitionSpec as P

HEADS = 8
CHUNKS = 2
AXIS = "narrow"
MESH = pl.DeviceIdType.MESH
F32 = jnp.float32
BF16 = jnp.bfloat16


def dot(a, b):
    return jnp.dot(a, b, preferred_element_type=F32)


def dot_nt(a, b):
    return lax.dot_general(a, b, (((1,), (1,)), ((), ())), preferred_element_type=F32)


def kernel(
    n,
    len_ref,
    hist_hbm,
    query_hbm,
    bucket_hbm,
    wk_hbm,
    wq_hbm,
    table_ref,
    gain_ref,
    wo_hbm,
    out_ref,
    slots,
    bslots,
    query,
    wk,
    wq,
    wo,
    wkt,
    qa,
    gates,
    acc,
    load_sem,
    recv_sem,
    right_sem,
    left_sem,
    brecv_sem,
    bright_sem,
    bleft_sem,
):
    chunks, rows, width = slots.shape[1:]
    shard_rows = chunks * rows
    head = width // HEADS
    me = lax.axis_index(AXIS)
    has_left = me > 0
    has_right = me < n - 1
    barrier = pltpu.get_barrier_semaphore()

    @pl.when(has_left)
    def _():
        pl.semaphore_signal(barrier, inc=1, device_id={AXIS: me - 1}, device_id_type=MESH)

    @pl.when(has_right)
    def _():
        pl.semaphore_signal(barrier, inc=1, device_id={AXIS: me + 1}, device_id_type=MESH)

    own = [
        pltpu.make_async_copy(hist_hbm.at[0, pl.ds(c * rows, rows)], slots.at[me, c], recv_sem.at[me, c])
        for c in range(chunks)
    ]
    own_bucket = pltpu.make_async_copy(bucket_hbm, bslots.at[me], brecv_sem.at[me])
    loads = [
        pltpu.make_async_copy(src, dst, load_sem.at[k])
        for k, (src, dst) in enumerate(
            ((query_hbm.at[0], query), (wq_hbm, wq), (wk_hbm, wk), (wo_hbm, wo))
        )
    ]
    own_bucket.start()
    for copy in own:
        copy.start()
    for copy in loads:
        copy.start()

    def hop(src, dst, send_sem, recv_sem, target):
        return pltpu.make_async_remote_copy(
            src_ref=src,
            dst_ref=dst,
            send_sem=send_sem,
            recv_sem=recv_sem,
            device_id={AXIS: target},
            device_id_type=MESH,
        )

    def right(src, o, c):
        return hop(src, slots.at[o, c], right_sem.at[o, c], recv_sem.at[o, c], me + 1)

    def left(src, o, c):
        return hop(src, slots.at[o, c], left_sem.at[o, c], recv_sem.at[o, c], me - 1)

    def bright(src, o):
        return hop(src, bslots.at[o], bright_sem.at[o], brecv_sem.at[o], me + 1)

    def bleft(src, o):
        return hop(src, bslots.at[o], bleft_sem.at[o], brecv_sem.at[o], me - 1)

    pl.semaphore_wait(barrier, jnp.minimum(me, 1) + jnp.minimum(n - 1 - me, 1))

    @pl.when(has_right)
    def _():
        bright(bucket_hbm, me).start()
        for c in range(chunks):
            right(hist_hbm.at[0, pl.ds(c * rows, rows)], me, c).start()

    @pl.when(has_left)
    def _():
        bleft(bucket_hbm, me).start()
        for c in range(chunks):
            left(hist_hbm.at[0, pl.ds(c * rows, rows)], me, c).start()

    loads[0].wait()
    loads[1].wait()
    q_rows = query.shape[0]
    states = jax.nn.silu(dot(query[...], wq[:, :width])).astype(BF16)
    states = states * (0.5 / math.sqrt(head))
    lane = lax.broadcasted_iota(jnp.int32, (q_rows, 16), 1)
    for h in range(HEADS):
        qa[h, :, :head] = states[:, h * head : (h + 1) * head].astype(BF16)
        qa[h, :, head:] = (lane == h).astype(F32).astype(BF16)
    gates[...] = jax.nn.silu(dot(query[...], wq[:, width:]))
    acc[...] = jnp.zeros_like(acc)
    loads[2].wait()
    wkt[...] = wk[:, :width].T
    length = len_ref[0]

    symmetric = jnp.minimum(me, n - 1 - me)
    side = jnp.where(me < n - 1 - me, 1, -1)

    def step(t, carry):
        i = t // chunks
        c = t % chunks
        near = jnp.where(i % 2 == 1, -((i + 1) // 2), (i + 1) // 2)
        o = me + jnp.where(i <= 2 * symmetric, near, side * (i - symmetric))

        @pl.when(c == 0)
        def _():
            pltpu.make_async_copy(bucket_hbm, bslots.at[o], brecv_sem.at[o]).wait()

            @pl.when((o < me) & has_right)
            def _():
                bright(bslots.at[o], o).start()

            @pl.when((o > me) & has_left)
            def _():
                bleft(bslots.at[o], o).start()

        pltpu.make_async_copy(hist_hbm.at[0, pl.ds(0, rows)], slots.at[o, c], recv_sem.at[o, c]).wait()

        @pl.when((o < me) & has_right)
        def _():
            right(slots.at[o, c], o, c).start()

        @pl.when((o > me) & has_left)
        def _():
            left(slots.at[o, c], o, c).start()

        x = slots[o, c]
        keys = jax.nn.silu(dot_nt(wkt[...], x)).astype(BF16)
        values = dot(x, wk[:, width:])
        position = o * shard_rows + c * rows + lax.broadcasted_iota(jnp.int32, (rows, 1), 0)
        values = jnp.where(position < length, values, 0.0).astype(BF16)
        bucket = bslots[o, :, pl.ds(pl.multiple_of(c * rows, rows), rows)]
        onehot = lax.broadcasted_iota(jnp.int32, (table_ref.shape[1], rows), 0) == bucket
        bias = dot(table_ref[...], onehot.astype(F32).astype(BF16)).astype(BF16)
        vlane = lax.broadcasted_iota(jnp.int32, (rows, 2 * head), 1)
        for p in range(HEADS // 2):
            pair = values[:, 2 * p * head : 2 * (p + 1) * head]
            zero = jnp.zeros_like(pair)
            total = None
            for k in range(2):
                h = 2 * p + k
                keys_h = jnp.concatenate([keys[h * head : (h + 1) * head], bias], axis=0)
                half = dot(qa[h], keys_h)
                weights = (half + half * jnp.tanh(half)).astype(BF16)
                mine = jnp.where((vlane < head) if k == 0 else (vlane >= head), pair, zero)
                term = dot(weights, mine)
                total = term if total is None else total + term
            acc[:, 2 * p * head : 2 * (p + 1) * head] += total
        return carry

    lax.fori_loop(0, n * chunks, step, 0)

    loads[3].wait()
    attended = acc[...]
    center = jnp.mean(attended, axis=-1, keepdims=True)
    shifted = attended - center
    spread = jnp.mean(jnp.square(shifted), axis=-1, keepdims=True)
    normed = shifted * lax.rsqrt(spread + 1e-05)
    mixed = (normed * gain_ref[...] * gates[...]).astype(BF16)
    out_ref[...] = (query[...].astype(F32) + dot(mixed, wo[...])).astype(BF16)

    def drain(o, carry):
        @pl.when((o <= me) & has_right)
        def _():
            bright(bslots.at[o], o).wait_send()
            for c in range(chunks):
                right(slots.at[o, c], o, c).wait_send()

        @pl.when((o >= me) & has_left)
        def _():
            bleft(bslots.at[o], o).wait_send()
            for c in range(chunks):
                left(slots.at[o, c], o, c).wait_send()

        return carry

    lax.fori_loop(0, n, drain, 0)


def on_device(
    n,
    hist_events,
    query_events,
    hist_lengths,
    time_buckets,
    w_key,
    w_query,
    bias_table,
    out_gain,
    w_out,
):
    shard_rows, width = hist_events.shape[1:]
    q_rows = query_events.shape[1]
    rows = shard_rows // CHUNKS
    buckets = bias_table.shape[0]
    table = jnp.pad(0.5 * bias_table.T, ((0, 16 - HEADS), (0, 0))).astype(BF16)
    anywhere = pl.BlockSpec(memory_space=pl.ANY)
    vmem = pl.BlockSpec(memory_space=pltpu.VMEM)
    dma = pltpu.SemaphoreType.DMA
    result = pl.pallas_call(
        functools.partial(kernel, n),
        out_shape=jax.ShapeDtypeStruct((q_rows, width), BF16),
        in_specs=[pl.BlockSpec(memory_space=pltpu.SMEM)]
        + [anywhere] * 5
        + [vmem, vmem, anywhere],
        out_specs=vmem,
        scratch_shapes=[
            pltpu.VMEM((n, CHUNKS, rows, width), BF16),
            pltpu.VMEM((n, 1, shard_rows), jnp.int32),
            pltpu.VMEM((q_rows, width), BF16),
            pltpu.VMEM(w_key.shape, BF16),
            pltpu.VMEM(w_query.shape, BF16),
            pltpu.VMEM(w_out.shape, BF16),
            pltpu.VMEM((width, width), BF16),
            pltpu.VMEM((HEADS, q_rows, width // HEADS + 16), BF16),
            pltpu.VMEM((q_rows, width), F32),
            pltpu.VMEM((q_rows, width), F32),
            dma((4,)),
            dma((n, CHUNKS)),
            dma((n, CHUNKS)),
            dma((n, CHUNKS)),
            dma((n,)),
            dma((n,)),
            dma((n,)),
        ],
        compiler_params=pltpu.CompilerParams(
            collective_id=0, has_side_effects=True, vmem_limit_bytes=60 * 1024 * 1024
        ),
    )(
        hist_lengths,
        hist_events,
        query_events,
        time_buckets,
        w_key,
        w_query,
        table,
        out_gain[None],
        w_out,
    )
    return result[None]


def solution(mesh):
    in_specs = (
        P(("parts", "wide"), AXIS, None),
        P(("parts", "wide"), AXIS, None),
        P(("parts", "wide")),
        P(("parts", "wide"), AXIS),
        P(),
        P(),
        P(),
        P(),
        P(),
    )
    out_specs = P(("parts", "wide"), AXIS, None)
    return jax.shard_map(
        functools.partial(on_device, mesh.shape[AXIS]),
        mesh=mesh,
        in_specs=in_specs,
        out_specs=out_specs,
        check_vma=False,
    )
```

```python
import functools
import math

import jax
import jax.numpy as jnp
from jax import lax
from jax.experimental import pallas as pl
from jax.experimental.pallas import tpu as pltpu
from jax.sharding import PartitionSpec as P

HEADS = 8
CHUNKS = 4
AXIS = "narrow"
MESH = pl.DeviceIdType.MESH
F32 = jnp.float32
BF16 = jnp.bfloat16


def dot(a, b):
    return jnp.dot(a, b, preferred_element_type=F32)


def dot_nt(a, b):
    return lax.dot_general(a, b, (((1,), (1,)), ((), ())), preferred_element_type=F32)


def kernel(
    n,
    len_ref,
    hist_hbm,
    query_hbm,
    bucket_hbm,
    wk_hbm,
    wq_hbm,
    table_ref,
    gain_ref,
    wo_hbm,
    out_ref,
    slots,
    bslots,
    query,
    wk,
    wq,
    wo,
    wkt,
    qa,
    gates,
    acc,
    load_sem,
    recv_sem,
    right_sem,
    left_sem,
    brecv_sem,
    bright_sem,
    bleft_sem,
    far_query,
    far_qa,
    far_acc,
    part_out,
    part_in,
    far_sem,
):
    chunks, rows, width = slots.shape[1:]
    shard_rows = chunks * rows
    head = width // HEADS
    me = lax.axis_index(AXIS)
    has_left = me > 0
    has_right = me < n - 1
    helping = n >= 4
    is_end = ((me == 0) | (me == n - 1)) & helping
    is_helper = ((me == 1) | (me == n - 2)) & helping
    low = me < n // 2
    helped = jnp.where(low, 2, n - 3)
    end = jnp.where(low, 0, n - 1)
    helper = jnp.where(low, 1, n - 2)
    barrier = pltpu.get_barrier_semaphore()

    @pl.when(has_left)
    def _():
        pl.semaphore_signal(barrier, inc=1, device_id={AXIS: me - 1}, device_id_type=MESH)

    @pl.when(has_right)
    def _():
        pl.semaphore_signal(barrier, inc=1, device_id={AXIS: me + 1}, device_id_type=MESH)

    own = [
        pltpu.make_async_copy(hist_hbm.at[0, pl.ds(c * rows, rows)], slots.at[me, c], recv_sem.at[me, c])
        for c in range(chunks)
    ]
    own_bucket = pltpu.make_async_copy(bucket_hbm, bslots.at[me], brecv_sem.at[me])
    loads = [
        pltpu.make_async_copy(src, dst, load_sem.at[k])
        for k, (src, dst) in enumerate(
            ((query_hbm.at[0], query), (wq_hbm, wq), (wk_hbm, wk), (wo_hbm, wo))
        )
    ]
    own_bucket.start()
    for copy in own:
        copy.start()
    for copy in loads:
        copy.start()

    def hop(src, dst, send_sem, recv_sem, target):
        return pltpu.make_async_remote_copy(
            src_ref=src,
            dst_ref=dst,
            send_sem=send_sem,
            recv_sem=recv_sem,
            device_id={AXIS: target},
            device_id_type=MESH,
        )

    def right(src, o, c):
        return hop(src, slots.at[o, c], right_sem.at[o, c], recv_sem.at[o, c], me + 1)

    def left(src, o, c):
        return hop(src, slots.at[o, c], left_sem.at[o, c], recv_sem.at[o, c], me - 1)

    def bright(src, o):
        return hop(src, bslots.at[o], bright_sem.at[o], brecv_sem.at[o], me + 1)

    def bleft(src, o):
        return hop(src, bslots.at[o], bleft_sem.at[o], brecv_sem.at[o], me - 1)

    pl.semaphore_wait(barrier, jnp.minimum(me, 1) + jnp.minimum(n - 1 - me, 1))

    far_send = hop(query_hbm.at[0], far_query, far_sem.at[0], far_sem.at[1], helper)
    part_send = hop(part_out, part_in, far_sem.at[2], far_sem.at[3], end)

    @pl.when(is_end)
    def _():
        far_send.start()

    @pl.when(has_right)
    def _():
        bright(bucket_hbm, me).start()
        for c in range(chunks):
            right(hist_hbm.at[0, pl.ds(c * rows, rows)], me, c).start()

    @pl.when(has_left)
    def _():
        bleft(bucket_hbm, me).start()
        for c in range(chunks):
            left(hist_hbm.at[0, pl.ds(c * rows, rows)], me, c).start()

    loads[0].wait()
    loads[1].wait()
    q_rows = query.shape[0]
    lane = lax.broadcasted_iota(jnp.int32, (q_rows, 16), 1)

    def project(events, target):
        states = jax.nn.silu(dot(events[...], wq[:, :width])).astype(BF16)
        states = states * (0.5 / math.sqrt(head))
        for h in range(HEADS):
            target[h, :, :head] = states[:, h * head : (h + 1) * head].astype(BF16)
            target[h, :, head:] = (lane == h).astype(F32).astype(BF16)

    project(query, qa)
    gates[...] = jax.nn.silu(dot(query[...], wq[:, width:]))
    acc[...] = jnp.zeros_like(acc)
    loads[2].wait()
    wkt[...] = wk[:, :width].T
    length = len_ref[0]
    eye = lax.broadcasted_iota(jnp.int32, (16, HEADS), 0) == lax.broadcasted_iota(jnp.int32, (16, HEADS), 1)
    half_eye = jnp.where(eye, 0.5, 0.0).astype(BF16)
    buckets = table_ref.shape[1]
    table = dot(half_eye, table_ref[...]).astype(BF16)

    def attend(states, sums, keys, values, bias):
        zero = jnp.zeros((rows, 2 * head), BF16)
        vlane = lax.broadcasted_iota(jnp.int32, (rows, 2 * head), 1)
        for p in range(HEADS // 2):
            pair = values[:, 2 * p * head : 2 * (p + 1) * head]
            total = None
            for k in range(2):
                h = 2 * p + k
                keys_h = jnp.concatenate([keys[h * head : (h + 1) * head], bias], axis=0)
                half = dot(states[h], keys_h)
                weights = (half + half * jnp.tanh(half)).astype(BF16)
                mine = jnp.where((vlane < head) if k == 0 else (vlane >= head), pair, zero)
                term = dot(weights, mine)
                total = term if total is None else total + term
            sums[:, 2 * p * head : 2 * (p + 1) * head] += total

    symmetric = jnp.minimum(me, n - 1 - me)
    side = jnp.where(low, 1, -1)

    def goes_right(o):
        return (o <= me) & has_right & jnp.logical_not(is_helper & (me >= n // 2) & (o == helped))

    def goes_left(o):
        return (o >= me) & has_left & jnp.logical_not(is_helper & (me < n // 2) & (o == helped))

    def step(t, carry):
        i = t // chunks
        c = t % chunks
        near = side * jnp.where(i % 2 == 1, (i + 1) // 2, -((i + 1) // 2))
        beyond = side * (i - symmetric + jnp.where(is_end & (i >= 2), 1, 0))
        o = me + jnp.where(i <= 2 * symmetric, near, beyond)

        @pl.when(c == 0)
        def _():
            pltpu.make_async_copy(bucket_hbm, bslots.at[o], brecv_sem.at[o]).wait()

            @pl.when(goes_right(o) & (o < me))
            def _():
                bright(bslots.at[o], o).start()

            @pl.when(goes_left(o) & (o > me))
            def _():
                bleft(bslots.at[o], o).start()

        pltpu.make_async_copy(hist_hbm.at[0, pl.ds(0, rows)], slots.at[o, c], recv_sem.at[o, c]).wait()

        @pl.when(goes_right(o) & (o < me))
        def _():
            right(slots.at[o, c], o, c).start()

        @pl.when(goes_left(o) & (o > me))
        def _():
            left(slots.at[o, c], o, c).start()

        @pl.when(is_helper & (t == 2 * chunks))
        def _():
            part_send.start()

        x = slots[o, c]
        keys = jax.nn.silu(dot_nt(wkt[...], x)).astype(BF16)
        values = dot(x, wk[:, width:])
        position = o * shard_rows + c * rows + lax.broadcasted_iota(jnp.int32, (rows, 1), 0)
        values = jnp.where(position < length, values, 0.0).astype(BF16)
        bucket = bslots[o, :, pl.ds(pl.multiple_of(c * rows, rows), rows)]
        onehot = lax.broadcasted_iota(jnp.int32, (buckets, rows), 0) == bucket
        bias = dot(table, onehot.astype(F32).astype(BF16)).astype(BF16)
        attend(qa, acc, keys, values, bias)

        @pl.when(is_helper & (o == helped))
        def _():
            @pl.when(c == 0)
            def _():
                far_send.wait_recv()
                project(far_query, far_qa)
                far_acc[...] = jnp.zeros_like(far_acc)

            attend(far_qa, far_acc, keys, values, bias)

            @pl.when(c == chunks - 1)
            def _():
                part_out[...] = far_acc[...].astype(BF16)

        return carry

    lax.fori_loop(0, (n - jnp.where(is_end, 1, 0)) * chunks, step, 0)

    @pl.when(is_end)
    def _():
        part_send.wait_recv()
        acc[...] += part_in[...].astype(F32)
        far_send.wait_send()

    @pl.when(is_helper)
    def _():
        part_send.wait_send()

    loads[3].wait()
    attended = acc[...]
    center = jnp.mean(attended, axis=-1, keepdims=True)
    shifted = attended - center
    spread = jnp.mean(jnp.square(shifted), axis=-1, keepdims=True)
    normed = shifted * lax.rsqrt(spread + 1e-05)
    mixed = (normed * gain_ref[...] * gates[...]).astype(BF16)
    out_ref[...] = (query[...].astype(F32) + dot(mixed, wo[...])).astype(BF16)

    def drain(o, carry):
        @pl.when(goes_right(o))
        def _():
            bright(bslots.at[o], o).wait_send()
            for c in range(chunks):
                right(slots.at[o, c], o, c).wait_send()

        @pl.when(goes_left(o))
        def _():
            bleft(bslots.at[o], o).wait_send()
            for c in range(chunks):
                left(slots.at[o, c], o, c).wait_send()

        return carry

    lax.fori_loop(0, n, drain, 0)


def on_device(
    n,
    hist_events,
    query_events,
    hist_lengths,
    time_buckets,
    w_key,
    w_query,
    bias_table,
    out_gain,
    w_out,
):
    shard_rows, width = hist_events.shape[1:]
    q_rows = query_events.shape[1]
    rows = shard_rows // CHUNKS
    anywhere = pl.BlockSpec(memory_space=pl.ANY)
    vmem = pl.BlockSpec(memory_space=pltpu.VMEM)
    dma = pltpu.SemaphoreType.DMA
    result = pl.pallas_call(
        functools.partial(kernel, n),
        out_shape=jax.ShapeDtypeStruct((q_rows, width), BF16),
        in_specs=[pl.BlockSpec(memory_space=pltpu.SMEM)]
        + [anywhere] * 5
        + [vmem, vmem, anywhere],
        out_specs=vmem,
        scratch_shapes=[
            pltpu.VMEM((n, CHUNKS, rows, width), BF16),
            pltpu.VMEM((n, 1, shard_rows), jnp.int32),
            pltpu.VMEM((q_rows, width), BF16),
            pltpu.VMEM(w_key.shape, BF16),
            pltpu.VMEM(w_query.shape, BF16),
            pltpu.VMEM(w_out.shape, BF16),
            pltpu.VMEM((width, width), BF16),
            pltpu.VMEM((HEADS, q_rows, width // HEADS + 16), BF16),
            pltpu.VMEM((q_rows, width), F32),
            pltpu.VMEM((q_rows, width), F32),
            dma((4,)),
            dma((n, CHUNKS)),
            dma((n, CHUNKS)),
            dma((n, CHUNKS)),
            dma((n,)),
            dma((n,)),
            dma((n,)),
            pltpu.VMEM((q_rows, width), BF16),
            pltpu.VMEM((HEADS, q_rows, width // HEADS + 16), BF16),
            pltpu.VMEM((q_rows, width), F32),
            pltpu.VMEM((q_rows, width), BF16),
            pltpu.VMEM((q_rows, width), BF16),
            dma((4,)),
        ],
        compiler_params=pltpu.CompilerParams(
            collective_id=0, has_side_effects=True, vmem_limit_bytes=60 * 1024 * 1024
        ),
    )(
        hist_lengths,
        hist_events,
        query_events,
        time_buckets,
        w_key,
        w_query,
        bias_table.T,
        out_gain[None],
        w_out,
    )
    return result[None]


def solution(mesh):
    in_specs = (
        P(("parts", "wide"), AXIS, None),
        P(("parts", "wide"), AXIS, None),
        P(("parts", "wide")),
        P(("parts", "wide"), AXIS),
        P(),
        P(),
        P(),
        P(),
        P(),
    )
    out_specs = P(("parts", "wide"), AXIS, None)
    return jax.shard_map(
        functools.partial(on_device, mesh.shape[AXIS]),
        mesh=mesh,
        in_specs=in_specs,
        out_specs=out_specs,
        check_vma=False,
    )
```

```python
import functools
import math

import jax
import jax.numpy as jnp
from jax import lax
from jax.experimental import pallas as pl
from jax.experimental.pallas import tpu as pltpu
from jax.sharding import PartitionSpec as P

HEADS = 8
CHUNKS = 4
AXIS = "narrow"
MESH = pl.DeviceIdType.MESH
F32 = jnp.float32
BF16 = jnp.bfloat16


def dot(a, b):
    return jnp.dot(a, b, preferred_element_type=F32)


def dot_nt(a, b):
    return lax.dot_general(a, b, (((1,), (1,)), ((), ())), preferred_element_type=F32)


def kernel(
    n,
    len_ref,
    hist_hbm,
    query_hbm,
    bucket_hbm,
    wk_hbm,
    wq_hbm,
    table_ref,
    gain_ref,
    wo_hbm,
    out_ref,
    slots,
    bslots,
    query,
    wk,
    wq,
    wo,
    wkt,
    qa,
    gates,
    acc,
    load_sem,
    recv_sem,
    right_sem,
    left_sem,
    brecv_sem,
    bright_sem,
    bleft_sem,
    far_query,
    far_qa,
    far_acc,
    part_out,
    part_in,
    far_sem,
):
    chunks, rows, width = slots.shape[1:]
    shard_rows = chunks * rows
    head = width // HEADS
    me = lax.axis_index(AXIS)
    has_left = me > 0
    has_right = me < n - 1
    helping = n >= 4
    is_end = ((me == 0) | (me == n - 1)) & helping
    is_helper = ((me == 1) | (me == n - 2)) & helping
    low = me < n // 2
    helped = jnp.where(low, 2, n - 3)
    end = jnp.where(low, 0, n - 1)
    helper = jnp.where(low, 1, n - 2)
    barrier = pltpu.get_barrier_semaphore()

    @pl.when(has_left)
    def _():
        pl.semaphore_signal(barrier, inc=1, device_id={AXIS: me - 1}, device_id_type=MESH)

    @pl.when(has_right)
    def _():
        pl.semaphore_signal(barrier, inc=1, device_id={AXIS: me + 1}, device_id_type=MESH)

    own = [
        pltpu.make_async_copy(hist_hbm.at[0, pl.ds(c * rows, rows)], slots.at[me, c], recv_sem.at[me, c])
        for c in range(chunks)
    ]
    own_bucket = pltpu.make_async_copy(bucket_hbm, bslots.at[me], brecv_sem.at[me])
    loads = [
        pltpu.make_async_copy(src, dst, load_sem.at[k])
        for k, (src, dst) in enumerate(
            ((query_hbm.at[0], query), (wq_hbm, wq), (wk_hbm, wk), (wo_hbm, wo))
        )
    ]
    own_bucket.start()
    for copy in own:
        copy.start()
    for copy in loads:
        copy.start()

    def hop(src, dst, send_sem, recv_sem, target):
        return pltpu.make_async_remote_copy(
            src_ref=src,
            dst_ref=dst,
            send_sem=send_sem,
            recv_sem=recv_sem,
            device_id={AXIS: target},
            device_id_type=MESH,
        )

    def right(src, o, c):
        return hop(src, slots.at[o, c], right_sem.at[o, c], recv_sem.at[o, c], me + 1)

    def left(src, o, c):
        return hop(src, slots.at[o, c], left_sem.at[o, c], recv_sem.at[o, c], me - 1)

    def bright(src, o):
        return hop(src, bslots.at[o], bright_sem.at[o], brecv_sem.at[o], me + 1)

    def bleft(src, o):
        return hop(src, bslots.at[o], bleft_sem.at[o], brecv_sem.at[o], me - 1)

    pl.semaphore_wait(barrier, jnp.minimum(me, 1) + jnp.minimum(n - 1 - me, 1))

    far_send = hop(query_hbm.at[0], far_query, far_sem.at[0], far_sem.at[1], helper)
    part_send = hop(part_out, part_in, far_sem.at[2], far_sem.at[3], end)

    @pl.when(is_end)
    def _():
        far_send.start()

    @pl.when(has_right)
    def _():
        bright(bucket_hbm, me).start()
        for c in range(chunks):
            right(hist_hbm.at[0, pl.ds(c * rows, rows)], me, c).start()

    @pl.when(has_left)
    def _():
        bleft(bucket_hbm, me).start()
        for c in range(chunks):
            left(hist_hbm.at[0, pl.ds(c * rows, rows)], me, c).start()

    loads[0].wait()
    loads[1].wait()
    q_rows = query.shape[0]
    lane = lax.broadcasted_iota(jnp.int32, (q_rows, 16), 1)

    def project(events, target):
        states = jax.nn.silu(dot(events[...], wq[:, :width])).astype(BF16)
        states = states * (0.5 / math.sqrt(head))
        for h in range(HEADS):
            target[h, :, :head] = states[:, h * head : (h + 1) * head].astype(BF16)
            target[h, :, head:] = (lane == h).astype(F32).astype(BF16)

    project(query, qa)
    gates[...] = jax.nn.silu(dot(query[...], wq[:, width:]))
    acc[...] = jnp.zeros_like(acc)
    loads[2].wait()
    wkt[...] = wk[:, :width].T
    length = len_ref[0]
    eye = lax.broadcasted_iota(jnp.int32, (16, HEADS), 0) == lax.broadcasted_iota(jnp.int32, (16, HEADS), 1)
    half_eye = jnp.where(eye, 0.5, 0.0).astype(BF16)
    buckets = table_ref.shape[1]
    table = dot(half_eye, table_ref[...]).astype(BF16)

    def attend(states, sums, keys, values, bias, pairs):
        zero = jnp.zeros((rows, 2 * head), BF16)
        vlane = lax.broadcasted_iota(jnp.int32, (rows, 2 * head), 1)
        for p in pairs:
            pair = values[:, 2 * p * head : 2 * (p + 1) * head]
            total = None
            for k in range(2):
                h = 2 * p + k
                keys_h = jnp.concatenate([keys[h * head : (h + 1) * head], bias], axis=0)
                half = dot(states[h], keys_h)
                weights = (half + half * jnp.tanh(half)).astype(BF16)
                mine = jnp.where((vlane < head) if k == 0 else (vlane >= head), pair, zero)
                term = dot(weights, mine)
                total = term if total is None else total + term
            sums[:, 2 * p * head : 2 * (p + 1) * head] += total

    symmetric = jnp.minimum(me, n - 1 - me)
    side = jnp.where(low, 1, -1)

    def goes_right(o):
        return (o <= me) & has_right & jnp.logical_not(is_helper & (me >= n // 2) & (o == helped))

    def goes_left(o):
        return (o >= me) & has_left & jnp.logical_not(is_helper & (me < n // 2) & (o == helped))

    def step(t, carry):
        i = t // chunks
        c = t % chunks
        near = side * jnp.where(i % 2 == 1, (i + 1) // 2, -((i + 1) // 2))
        beyond = side * (i - symmetric + jnp.where(is_end & (i >= 2), 1, 0))
        o = me + jnp.where(i <= 2 * symmetric, near, beyond)

        @pl.when(c == 0)
        def _():
            pltpu.make_async_copy(bucket_hbm, bslots.at[o], brecv_sem.at[o]).wait()

            @pl.when(goes_right(o) & (o < me))
            def _():
                bright(bslots.at[o], o).start()

            @pl.when(goes_left(o) & (o > me))
            def _():
                bleft(bslots.at[o], o).start()

        pltpu.make_async_copy(hist_hbm.at[0, pl.ds(0, rows)], slots.at[o, c], recv_sem.at[o, c]).wait()

        @pl.when(goes_right(o) & (o < me))
        def _():
            right(slots.at[o, c], o, c).start()

        @pl.when(goes_left(o) & (o > me))
        def _():
            left(slots.at[o, c], o, c).start()

        x = slots[o, c]
        keys = jax.nn.silu(dot_nt(wkt[...], x)).astype(BF16)
        values = dot(x, wk[:, width:])
        position = o * shard_rows + c * rows + lax.broadcasted_iota(jnp.int32, (rows, 1), 0)
        values = jnp.where(position < length, values, 0.0).astype(BF16)
        bucket = bslots[o, :, pl.ds(pl.multiple_of(c * rows, rows), rows)]
        onehot = lax.broadcasted_iota(jnp.int32, (buckets, rows), 0) == bucket
        bias = dot(table, onehot.astype(F32).astype(BF16)).astype(BF16)

        @pl.when(is_helper & (o == helped))
        def _():
            @pl.when(c == 0)
            def _():
                far_send.wait_recv()
                project(far_query, far_qa)
                far_acc[...] = jnp.zeros_like(far_acc)

            attend(far_qa, far_acc, keys, values, bias, range(HEADS // 2))

            @pl.when(c == chunks - 1)
            def _():
                part_out[...] = far_acc[...].astype(BF16)

        attend(qa, acc, keys, values, bias, range(1))

        @pl.when(is_helper & (o == helped) & (c == chunks - 1))
        def _():
            part_send.start()

        attend(qa, acc, keys, values, bias, range(1, HEADS // 2))
        return carry

    lax.fori_loop(0, (n - jnp.where(is_end, 1, 0)) * chunks, step, 0)

    @pl.when(is_end)
    def _():
        part_send.wait_recv()
        acc[...] += part_in[...].astype(F32)
        far_send.wait_send()

    @pl.when(is_helper)
    def _():
        part_send.wait_send()

    loads[3].wait()
    attended = acc[...]
    center = jnp.mean(attended, axis=-1, keepdims=True)
    shifted = attended - center
    spread = jnp.mean(jnp.square(shifted), axis=-1, keepdims=True)
    normed = shifted * lax.rsqrt(spread + 1e-05)
    mixed = (normed * gain_ref[...] * gates[...]).astype(BF16)
    out_ref[...] = (query[...].astype(F32) + dot(mixed, wo[...])).astype(BF16)

    def drain(o, carry):
        @pl.when(goes_right(o))
        def _():
            bright(bslots.at[o], o).wait_send()
            for c in range(chunks):
                right(slots.at[o, c], o, c).wait_send()

        @pl.when(goes_left(o))
        def _():
            bleft(bslots.at[o], o).wait_send()
            for c in range(chunks):
                left(slots.at[o, c], o, c).wait_send()

        return carry

    lax.fori_loop(0, n, drain, 0)


def on_device(
    n,
    hist_events,
    query_events,
    hist_lengths,
    time_buckets,
    w_key,
    w_query,
    bias_table,
    out_gain,
    w_out,
):
    shard_rows, width = hist_events.shape[1:]
    q_rows = query_events.shape[1]
    rows = shard_rows // CHUNKS
    anywhere = pl.BlockSpec(memory_space=pl.ANY)
    vmem = pl.BlockSpec(memory_space=pltpu.VMEM)
    dma = pltpu.SemaphoreType.DMA
    result = pl.pallas_call(
        functools.partial(kernel, n),
        out_shape=jax.ShapeDtypeStruct((q_rows, width), BF16),
        in_specs=[pl.BlockSpec(memory_space=pltpu.SMEM)]
        + [anywhere] * 5
        + [vmem, vmem, anywhere],
        out_specs=vmem,
        scratch_shapes=[
            pltpu.VMEM((n, CHUNKS, rows, width), BF16),
            pltpu.VMEM((n, 1, shard_rows), jnp.int32),
            pltpu.VMEM((q_rows, width), BF16),
            pltpu.VMEM(w_key.shape, BF16),
            pltpu.VMEM(w_query.shape, BF16),
            pltpu.VMEM(w_out.shape, BF16),
            pltpu.VMEM((width, width), BF16),
            pltpu.VMEM((HEADS, q_rows, width // HEADS + 16), BF16),
            pltpu.VMEM((q_rows, width), F32),
            pltpu.VMEM((q_rows, width), F32),
            dma((4,)),
            dma((n, CHUNKS)),
            dma((n, CHUNKS)),
            dma((n, CHUNKS)),
            dma((n,)),
            dma((n,)),
            dma((n,)),
            pltpu.VMEM((q_rows, width), BF16),
            pltpu.VMEM((HEADS, q_rows, width // HEADS + 16), BF16),
            pltpu.VMEM((q_rows, width), F32),
            pltpu.VMEM((q_rows, width), BF16),
            pltpu.VMEM((q_rows, width), BF16),
            dma((4,)),
        ],
        compiler_params=pltpu.CompilerParams(
            collective_id=0, has_side_effects=True, vmem_limit_bytes=60 * 1024 * 1024
        ),
    )(
        hist_lengths,
        hist_events,
        query_events,
        time_buckets,
        w_key,
        w_query,
        bias_table.T,
        out_gain[None],
        w_out,
    )
    return result[None]


def solution(mesh):
    in_specs = (
        P(("parts", "wide"), AXIS, None),
        P(("parts", "wide"), AXIS, None),
        P(("parts", "wide")),
        P(("parts", "wide"), AXIS),
        P(),
        P(),
        P(),
        P(),
        P(),
    )
    out_specs = P(("parts", "wide"), AXIS, None)
    return jax.shard_map(
        functools.partial(on_device, mesh.shape[AXIS]),
        mesh=mesh,
        in_specs=in_specs,
        out_specs=out_specs,
        check_vma=False,
    )
```

```python
import functools
import math

import jax
import jax.numpy as jnp
from jax import lax
from jax.experimental import pallas as pl
from jax.experimental.pallas import tpu as pltpu
from jax.sharding import PartitionSpec as P

HEADS = 8
CHUNKS = 4
AXIS = "narrow"
MESH = pl.DeviceIdType.MESH
F32 = jnp.float32
BF16 = jnp.bfloat16


def dot(a, b):
    return jnp.dot(a, b, preferred_element_type=F32)


def dot_nt(a, b):
    return lax.dot_general(a, b, (((1,), (1,)), ((), ())), preferred_element_type=F32)


def kernel(
    n,
    len_ref,
    hist_hbm,
    query_hbm,
    bucket_hbm,
    wk_hbm,
    wq_hbm,
    table_ref,
    gain_ref,
    out_ref,
    slots,
    bslots,
    query,
    wk,
    wq,
    wkt,
    qa,
    gates,
    acc,
    load_sem,
    recv_sem,
    right_sem,
    left_sem,
    brecv_sem,
    bright_sem,
    bleft_sem,
    far_query,
    far_qa,
    far_acc,
    part_out,
    part_in,
    far_sem,
):
    chunks, rows, width = slots.shape[1:]
    shard_rows = chunks * rows
    head = width // HEADS
    me = lax.axis_index(AXIS)
    has_left = me > 0
    has_right = me < n - 1
    helping = n >= 4
    is_end = ((me == 0) | (me == n - 1)) & helping
    is_helper = ((me == 1) | (me == n - 2)) & helping
    low = me < n // 2
    helped = jnp.where(low, 2, n - 3)
    end = jnp.where(low, 0, n - 1)
    helper = jnp.where(low, 1, n - 2)
    barrier = pltpu.get_barrier_semaphore()

    @pl.when(has_left)
    def _():
        pl.semaphore_signal(barrier, inc=1, device_id={AXIS: me - 1}, device_id_type=MESH)

    @pl.when(has_right)
    def _():
        pl.semaphore_signal(barrier, inc=1, device_id={AXIS: me + 1}, device_id_type=MESH)

    own = [
        pltpu.make_async_copy(hist_hbm.at[0, pl.ds(c * rows, rows)], slots.at[me, c], recv_sem.at[me, c])
        for c in range(chunks)
    ]
    own_bucket = pltpu.make_async_copy(bucket_hbm, bslots.at[me], brecv_sem.at[me])
    loads = [
        pltpu.make_async_copy(src, dst, load_sem.at[k])
        for k, (src, dst) in enumerate(
            ((query_hbm.at[0], query), (wq_hbm, wq), (wk_hbm, wk))
        )
    ]
    own_bucket.start()
    for copy in own:
        copy.start()
    for copy in loads:
        copy.start()

    def hop(src, dst, send_sem, recv_sem, target):
        return pltpu.make_async_remote_copy(
            src_ref=src,
            dst_ref=dst,
            send_sem=send_sem,
            recv_sem=recv_sem,
            device_id={AXIS: target},
            device_id_type=MESH,
        )

    def right(src, o, c):
        return hop(src, slots.at[o, c], right_sem.at[o, c], recv_sem.at[o, c], me + 1)

    def left(src, o, c):
        return hop(src, slots.at[o, c], left_sem.at[o, c], recv_sem.at[o, c], me - 1)

    def bright(src, o):
        return hop(src, bslots.at[o], bright_sem.at[o], brecv_sem.at[o], me + 1)

    def bleft(src, o):
        return hop(src, bslots.at[o], bleft_sem.at[o], brecv_sem.at[o], me - 1)

    pl.semaphore_wait(barrier, jnp.minimum(me, 1) + jnp.minimum(n - 1 - me, 1))

    far_send = hop(query_hbm.at[0], far_query, far_sem.at[0], far_sem.at[1], helper)
    part_send = hop(part_out, part_in, far_sem.at[2], far_sem.at[3], end)

    @pl.when(is_end)
    def _():
        far_send.start()

    @pl.when(has_right)
    def _():
        bright(bucket_hbm, me).start()
        for c in range(chunks):
            right(hist_hbm.at[0, pl.ds(c * rows, rows)], me, c).start()

    @pl.when(has_left)
    def _():
        bleft(bucket_hbm, me).start()
        for c in range(chunks):
            left(hist_hbm.at[0, pl.ds(c * rows, rows)], me, c).start()

    loads[0].wait()
    loads[1].wait()
    q_rows = query.shape[0]
    lane = lax.broadcasted_iota(jnp.int32, (q_rows, 16), 1)

    def project(events, target):
        states = jax.nn.silu(dot(events[...], wq[:, :width])).astype(BF16)
        states = states * (0.5 / math.sqrt(head))
        for h in range(HEADS):
            target[h, :, :head] = states[:, h * head : (h + 1) * head].astype(BF16)
            target[h, :, head:] = (lane == h).astype(F32).astype(BF16)

    project(query, qa)
    gates[...] = jax.nn.silu(dot(query[...], wq[:, width:]))
    acc[...] = jnp.zeros_like(acc)
    loads[2].wait()
    wkt[...] = wk[:, :width].T
    length = len_ref[0]
    eye = lax.broadcasted_iota(jnp.int32, (16, HEADS), 0) == lax.broadcasted_iota(jnp.int32, (16, HEADS), 1)
    half_eye = jnp.where(eye, 0.5, 0.0).astype(BF16)
    buckets = table_ref.shape[1]
    table = dot(half_eye, table_ref[...]).astype(BF16)

    def attend(states, sums, keys, values, bias, pairs):
        zero = jnp.zeros((rows, 2 * head), BF16)
        vlane = lax.broadcasted_iota(jnp.int32, (rows, 2 * head), 1)
        for p in pairs:
            pair = values[:, 2 * p * head : 2 * (p + 1) * head]
            total = None
            for k in range(2):
                h = 2 * p + k
                keys_h = jnp.concatenate([keys[h * head : (h + 1) * head], bias], axis=0)
                half = dot(states[h], keys_h)
                weights = (half + half * jnp.tanh(half)).astype(BF16)
                mine = jnp.where((vlane < head) if k == 0 else (vlane >= head), pair, zero)
                term = dot(weights, mine)
                total = term if total is None else total + term
            sums[:, 2 * p * head : 2 * (p + 1) * head] += total

    symmetric = jnp.minimum(me, n - 1 - me)
    side = jnp.where(low, 1, -1)

    def goes_right(o):
        return (o <= me) & has_right & jnp.logical_not(is_helper & (me >= n // 2) & (o == helped))

    def goes_left(o):
        return (o >= me) & has_left & jnp.logical_not(is_helper & (me < n // 2) & (o == helped))

    def step(t, carry):
        i = t // chunks
        c = t % chunks
        near = side * jnp.where(i % 2 == 1, (i + 1) // 2, -((i + 1) // 2))
        beyond = side * (i - symmetric + jnp.where(is_end & (i >= 2), 1, 0))
        o = me + jnp.where(i <= 2 * symmetric, near, beyond)

        @pl.when(c == 0)
        def _():
            pltpu.make_async_copy(bucket_hbm, bslots.at[o], brecv_sem.at[o]).wait()

            @pl.when(goes_right(o) & (o < me))
            def _():
                bright(bslots.at[o], o).start()

            @pl.when(goes_left(o) & (o > me))
            def _():
                bleft(bslots.at[o], o).start()

        pltpu.make_async_copy(hist_hbm.at[0, pl.ds(0, rows)], slots.at[o, c], recv_sem.at[o, c]).wait()

        @pl.when(goes_right(o) & (o < me))
        def _():
            right(slots.at[o, c], o, c).start()

        @pl.when(goes_left(o) & (o > me))
        def _():
            left(slots.at[o, c], o, c).start()

        x = slots[o, c]
        keys = jax.nn.silu(dot_nt(wkt[...], x)).astype(BF16)
        values = dot(x, wk[:, width:])
        position = o * shard_rows + c * rows + lax.broadcasted_iota(jnp.int32, (rows, 1), 0)
        values = jnp.where(position < length, values, 0.0).astype(BF16)
        bucket = bslots[o, :, pl.ds(pl.multiple_of(c * rows, rows), rows)]
        onehot = lax.broadcasted_iota(jnp.int32, (buckets, rows), 0) == bucket
        bias = dot(table, onehot.astype(F32).astype(BF16)).astype(BF16)

        @pl.when(is_helper & (o == helped))
        def _():
            @pl.when(c == 0)
            def _():
                far_send.wait_recv()
                project(far_query, far_qa)
                far_acc[...] = jnp.zeros_like(far_acc)

            attend(far_qa, far_acc, keys, values, bias, range(HEADS // 2))

            @pl.when(c == chunks - 1)
            def _():
                part_out[...] = far_acc[...].astype(BF16)

        attend(qa, acc, keys, values, bias, range(1))

        @pl.when(is_helper & (o == helped) & (c == chunks - 1))
        def _():
            part_send.start()

        attend(qa, acc, keys, values, bias, range(1, HEADS // 2))
        return carry

    lax.fori_loop(0, (n - jnp.where(is_end, 1, 0)) * chunks, step, 0)

    @pl.when(is_end)
    def _():
        part_send.wait_recv()
        acc[...] += part_in[...].astype(F32)
        far_send.wait_send()

    @pl.when(is_helper)
    def _():
        part_send.wait_send()

    attended = acc[...]
    center = jnp.mean(attended, axis=-1, keepdims=True)
    shifted = attended - center
    spread = jnp.mean(jnp.square(shifted), axis=-1, keepdims=True)
    normed = shifted * lax.rsqrt(spread + 1e-05)
    out_ref[...] = (normed * gain_ref[...] * gates[...]).astype(BF16)

    def drain(o, carry):
        @pl.when(goes_right(o))
        def _():
            bright(bslots.at[o], o).wait_send()
            for c in range(chunks):
                right(slots.at[o, c], o, c).wait_send()

        @pl.when(goes_left(o))
        def _():
            bleft(bslots.at[o], o).wait_send()
            for c in range(chunks):
                left(slots.at[o, c], o, c).wait_send()

        return carry

    lax.fori_loop(0, n, drain, 0)


def on_device(
    n,
    hist_events,
    query_events,
    hist_lengths,
    time_buckets,
    w_key,
    w_query,
    bias_table,
    out_gain,
    w_out,
):
    shard_rows, width = hist_events.shape[1:]
    q_rows = query_events.shape[1]
    rows = shard_rows // CHUNKS
    anywhere = pl.BlockSpec(memory_space=pl.ANY)
    vmem = pl.BlockSpec(memory_space=pltpu.VMEM)
    dma = pltpu.SemaphoreType.DMA
    mixed = pl.pallas_call(
        functools.partial(kernel, n),
        out_shape=jax.ShapeDtypeStruct((q_rows, width), BF16),
        in_specs=[pl.BlockSpec(memory_space=pltpu.SMEM)]
        + [anywhere] * 5
        + [vmem, vmem],
        out_specs=vmem,
        scratch_shapes=[
            pltpu.VMEM((n, CHUNKS, rows, width), BF16),
            pltpu.VMEM((n, 1, shard_rows), jnp.int32),
            pltpu.VMEM((q_rows, width), BF16),
            pltpu.VMEM(w_key.shape, BF16),
            pltpu.VMEM(w_query.shape, BF16),
            pltpu.VMEM((width, width), BF16),
            pltpu.VMEM((HEADS, q_rows, width // HEADS + 16), BF16),
            pltpu.VMEM((q_rows, width), F32),
            pltpu.VMEM((q_rows, width), F32),
            dma((3,)),
            dma((n, CHUNKS)),
            dma((n, CHUNKS)),
            dma((n, CHUNKS)),
            dma((n,)),
            dma((n,)),
            dma((n,)),
            pltpu.VMEM((q_rows, width), BF16),
            pltpu.VMEM((HEADS, q_rows, width // HEADS + 16), BF16),
            pltpu.VMEM((q_rows, width), F32),
            pltpu.VMEM((q_rows, width), BF16),
            pltpu.VMEM((q_rows, width), BF16),
            dma((4,)),
        ],
        compiler_params=pltpu.CompilerParams(
            collective_id=0, has_side_effects=True, vmem_limit_bytes=60 * 1024 * 1024
        ),
    )(
        hist_lengths,
        hist_events,
        query_events,
        time_buckets,
        w_key,
        w_query,
        bias_table.T,
        out_gain[None],
    )
    result = query_events[0].astype(F32) + dot(mixed, w_out)
    return result.astype(BF16)[None]


def solution(mesh):
    in_specs = (
        P(("parts", "wide"), AXIS, None),
        P(("parts", "wide"), AXIS, None),
        P(("parts", "wide")),
        P(("parts", "wide"), AXIS),
        P(),
        P(),
        P(),
        P(),
        P(),
    )
    out_specs = P(("parts", "wide"), AXIS, None)
    return jax.shard_map(
        functools.partial(on_device, mesh.shape[AXIS]),
        mesh=mesh,
        in_specs=in_specs,
        out_specs=out_specs,
        check_vma=False,
    )
```

```python
import functools
import math

import jax
import jax.numpy as jnp
from jax import lax
from jax.experimental import pallas as pl
from jax.experimental.pallas import tpu as pltpu
from jax.sharding import PartitionSpec as P

HEADS = 8
CHUNKS = 4
AXIS = "narrow"
MESH = pl.DeviceIdType.MESH
F32 = jnp.float32
BF16 = jnp.bfloat16


def dot(a, b):
    return jnp.dot(a, b, preferred_element_type=F32)


def dot_nt(a, b):
    return lax.dot_general(a, b, (((1,), (1,)), ((), ())), preferred_element_type=F32)


def kernel(
    n,
    len_ref,
    hist_hbm,
    query_hbm,
    bucket_hbm,
    wk_hbm,
    wq_hbm,
    table_ref,
    gain_ref,
    wo_hbm,
    out_ref,
    slots,
    bslots,
    query,
    wk,
    wq,
    wo,
    wkt,
    qa,
    gates,
    acc,
    load_sem,
    recv_sem,
    right_sem,
    left_sem,
    brecv_sem,
    bright_sem,
    bleft_sem,
    far_query,
    far_qa,
    far_acc,
    part_out,
    part_in,
    far_sem,
):
    chunks, rows, width = slots.shape[1:]
    shard_rows = chunks * rows
    head = width // HEADS
    me = lax.axis_index(AXIS)
    has_left = me > 0
    has_right = me < n - 1
    helping = n >= 4
    is_end = ((me == 0) | (me == n - 1)) & helping
    is_helper = ((me == 1) | (me == n - 2)) & helping
    low = me < n // 2
    helped = jnp.where(low, 2, n - 3)
    end = jnp.where(low, 0, n - 1)
    helper = jnp.where(low, 1, n - 2)
    barrier = pltpu.get_barrier_semaphore()

    @pl.when(has_left)
    def _():
        pl.semaphore_signal(barrier, inc=1, device_id={AXIS: me - 1}, device_id_type=MESH)

    @pl.when(has_right)
    def _():
        pl.semaphore_signal(barrier, inc=1, device_id={AXIS: me + 1}, device_id_type=MESH)

    own = [
        pltpu.make_async_copy(hist_hbm.at[0, pl.ds(c * rows, rows)], slots.at[me, c], recv_sem.at[me, c])
        for c in range(chunks)
    ]
    own_bucket = pltpu.make_async_copy(bucket_hbm, bslots.at[me], brecv_sem.at[me])
    loads = [
        pltpu.make_async_copy(src, dst, load_sem.at[k])
        for k, (src, dst) in enumerate(
            ((query_hbm.at[0], query), (wq_hbm, wq), (wk_hbm, wk), (wo_hbm, wo))
        )
    ]
    own_bucket.start()
    for copy in own:
        copy.start()
    for copy in loads:
        copy.start()

    def hop(src, dst, send_sem, recv_sem, target):
        return pltpu.make_async_remote_copy(
            src_ref=src,
            dst_ref=dst,
            send_sem=send_sem,
            recv_sem=recv_sem,
            device_id={AXIS: target},
            device_id_type=MESH,
        )

    def right(src, o, c):
        return hop(src, slots.at[o, c], right_sem.at[o, c], recv_sem.at[o, c], me + 1)

    def left(src, o, c):
        return hop(src, slots.at[o, c], left_sem.at[o, c], recv_sem.at[o, c], me - 1)

    def bright(src, o):
        return hop(src, bslots.at[o], bright_sem.at[o], brecv_sem.at[o], me + 1)

    def bleft(src, o):
        return hop(src, bslots.at[o], bleft_sem.at[o], brecv_sem.at[o], me - 1)

    pl.semaphore_wait(barrier, jnp.minimum(me, 1) + jnp.minimum(n - 1 - me, 1))

    far_send = hop(query_hbm.at[0], far_query, far_sem.at[0], far_sem.at[1], helper)
    part_send = hop(part_out, part_in, far_sem.at[2], far_sem.at[3], end)

    @pl.when(is_end)
    def _():
        far_send.start()

    @pl.when(has_right)
    def _():
        bright(bucket_hbm, me).start()
        for c in range(chunks):
            right(hist_hbm.at[0, pl.ds(c * rows, rows)], me, c).start()

    @pl.when(has_left)
    def _():
        bleft(bucket_hbm, me).start()
        for c in range(chunks):
            left(hist_hbm.at[0, pl.ds(c * rows, rows)], me, c).start()

    loads[0].wait()
    loads[1].wait()
    q_rows = query.shape[0]
    lane = lax.broadcasted_iota(jnp.int32, (q_rows, 16), 1)

    def project(events, target):
        states = jax.nn.silu(dot(events[...], wq[:, :width])).astype(BF16)
        states = states * (0.5 / math.sqrt(head))
        for h in range(HEADS):
            target[h, :, :head] = states[:, h * head : (h + 1) * head].astype(BF16)
            target[h, :, head:] = (lane == h).astype(F32).astype(BF16)

    project(query, qa)
    gates[...] = jax.nn.silu(dot(query[...], wq[:, width:]))
    acc[...] = jnp.zeros_like(acc)
    loads[2].wait()
    wkt[...] = wk[:, :width].T
    length = len_ref[0]
    eye = lax.broadcasted_iota(jnp.int32, (16, HEADS), 0) == lax.broadcasted_iota(jnp.int32, (16, HEADS), 1)
    half_eye = jnp.where(eye, 0.5, 0.0).astype(BF16)
    buckets = table_ref.shape[1]
    table = dot(half_eye, table_ref[...]).astype(BF16)

    def attend(states, sums, keys, values, bias, pairs):
        zero = jnp.zeros((rows, 2 * head), BF16)
        vlane = lax.broadcasted_iota(jnp.int32, (rows, 2 * head), 1)
        for p in pairs:
            pair = values[:, 2 * p * head : 2 * (p + 1) * head]
            total = None
            for k in range(2):
                h = 2 * p + k
                keys_h = jnp.concatenate([keys[h * head : (h + 1) * head], bias], axis=0)
                half = dot(states[h], keys_h)
                weights = (half + half * jnp.tanh(half)).astype(BF16)
                mine = jnp.where((vlane < head) if k == 0 else (vlane >= head), pair, zero)
                term = dot(weights, mine)
                total = term if total is None else total + term
            sums[:, 2 * p * head : 2 * (p + 1) * head] += total

    symmetric = jnp.minimum(me, n - 1 - me)
    side = jnp.where(low, 1, -1)

    def goes_right(o):
        return (o <= me) & has_right & jnp.logical_not(is_helper & (me >= n // 2) & (o == helped))

    def goes_left(o):
        return (o >= me) & has_left & jnp.logical_not(is_helper & (me < n // 2) & (o == helped))

    def step(t, carry):
        i = t // chunks
        c = t % chunks
        near = side * jnp.where(i % 2 == 1, (i + 1) // 2, -((i + 1) // 2))
        beyond = side * (i - symmetric + jnp.where(is_end & (i >= 2), 1, 0))
        o = me + jnp.where(i <= 2 * symmetric, near, beyond)

        @pl.when(c == 0)
        def _():
            pltpu.make_async_copy(bucket_hbm, bslots.at[o], brecv_sem.at[o]).wait()

            @pl.when(goes_right(o) & (o < me))
            def _():
                bright(bslots.at[o], o).start()

            @pl.when(goes_left(o) & (o > me))
            def _():
                bleft(bslots.at[o], o).start()

        def receive(block, piece):
            pltpu.make_async_copy(
                hist_hbm.at[0, pl.ds(0, rows)], slots.at[block, piece], recv_sem.at[block, piece]
            ).wait()

            @pl.when(goes_right(block) & (block < me))
            def _():
                right(slots.at[block, piece], block, piece).start()

            @pl.when(goes_left(block) & (block > me))
            def _():
                left(slots.at[block, piece], block, piece).start()

        @pl.when(is_helper & (i == 1) & (c >= 2))
        def _():
            receive(end, c - 2)

        @pl.when(jnp.logical_not(is_helper & (o == end) & (c < chunks - 2)))
        def _():
            receive(o, c)

        x = slots[o, c]
        keys = jax.nn.silu(dot_nt(wkt[...], x)).astype(BF16)
        values = dot(x, wk[:, width:])
        position = o * shard_rows + c * rows + lax.broadcasted_iota(jnp.int32, (rows, 1), 0)
        values = jnp.where(position < length, values, 0.0).astype(BF16)
        bucket = bslots[o, :, pl.ds(pl.multiple_of(c * rows, rows), rows)]
        onehot = lax.broadcasted_iota(jnp.int32, (buckets, rows), 0) == bucket
        bias = dot(table, onehot.astype(F32).astype(BF16)).astype(BF16)

        @pl.when(is_helper & (o == helped))
        def _():
            @pl.when(c == 0)
            def _():
                far_send.wait_recv()
                project(far_query, far_qa)
                far_acc[...] = jnp.zeros_like(far_acc)

            attend(far_qa, far_acc, keys, values, bias, range(HEADS // 2))

            @pl.when(c == chunks - 1)
            def _():
                part_out[...] = far_acc[...].astype(BF16)

        attend(qa, acc, keys, values, bias, range(1))

        @pl.when(is_helper & (o == helped) & (c == chunks - 1))
        def _():
            part_send.start()

        attend(qa, acc, keys, values, bias, range(1, HEADS // 2))
        return carry

    lax.fori_loop(0, (n - jnp.where(is_end, 1, 0)) * chunks, step, 0)

    @pl.when(is_end)
    def _():
        part_send.wait_recv()
        acc[...] += part_in[...].astype(F32)
        far_send.wait_send()

    @pl.when(is_helper)
    def _():
        part_send.wait_send()

    loads[3].wait()
    attended = acc[...]
    center = jnp.mean(attended, axis=-1, keepdims=True)
    shifted = attended - center
    spread = jnp.mean(jnp.square(shifted), axis=-1, keepdims=True)
    normed = shifted * lax.rsqrt(spread + 1e-05)
    mixed = (normed * gain_ref[...] * gates[...]).astype(BF16)
    out_ref[...] = (query[...].astype(F32) + dot(mixed, wo[...])).astype(BF16)

    def drain(o, carry):
        @pl.when(goes_right(o))
        def _():
            bright(bslots.at[o], o).wait_send()
            for c in range(chunks):
                right(slots.at[o, c], o, c).wait_send()

        @pl.when(goes_left(o))
        def _():
            bleft(bslots.at[o], o).wait_send()
            for c in range(chunks):
                left(slots.at[o, c], o, c).wait_send()

        return carry

    lax.fori_loop(0, n, drain, 0)


def on_device(
    n,
    hist_events,
    query_events,
    hist_lengths,
    time_buckets,
    w_key,
    w_query,
    bias_table,
    out_gain,
    w_out,
):
    shard_rows, width = hist_events.shape[1:]
    q_rows = query_events.shape[1]
    rows = shard_rows // CHUNKS
    anywhere = pl.BlockSpec(memory_space=pl.ANY)
    vmem = pl.BlockSpec(memory_space=pltpu.VMEM)
    dma = pltpu.SemaphoreType.DMA
    result = pl.pallas_call(
        functools.partial(kernel, n),
        out_shape=jax.ShapeDtypeStruct((q_rows, width), BF16),
        in_specs=[pl.BlockSpec(memory_space=pltpu.SMEM)]
        + [anywhere] * 5
        + [vmem, vmem, anywhere],
        out_specs=vmem,
        scratch_shapes=[
            pltpu.VMEM((n, CHUNKS, rows, width), BF16),
            pltpu.VMEM((n, 1, shard_rows), jnp.int32),
            pltpu.VMEM((q_rows, width), BF16),
            pltpu.VMEM(w_key.shape, BF16),
            pltpu.VMEM(w_query.shape, BF16),
            pltpu.VMEM(w_out.shape, BF16),
            pltpu.VMEM((width, width), BF16),
            pltpu.VMEM((HEADS, q_rows, width // HEADS + 16), BF16),
            pltpu.VMEM((q_rows, width), F32),
            pltpu.VMEM((q_rows, width), F32),
            dma((4,)),
            dma((n, CHUNKS)),
            dma((n, CHUNKS)),
            dma((n, CHUNKS)),
            dma((n,)),
            dma((n,)),
            dma((n,)),
            pltpu.VMEM((q_rows, width), BF16),
            pltpu.VMEM((HEADS, q_rows, width // HEADS + 16), BF16),
            pltpu.VMEM((q_rows, width), F32),
            pltpu.VMEM((q_rows, width), BF16),
            pltpu.VMEM((q_rows, width), BF16),
            dma((4,)),
        ],
        compiler_params=pltpu.CompilerParams(
            collective_id=0, has_side_effects=True, vmem_limit_bytes=60 * 1024 * 1024
        ),
    )(
        hist_lengths,
        hist_events,
        query_events,
        time_buckets,
        w_key,
        w_query,
        bias_table.T,
        out_gain[None],
        w_out,
    )
    return result[None]


def solution(mesh):
    in_specs = (
        P(("parts", "wide"), AXIS, None),
        P(("parts", "wide"), AXIS, None),
        P(("parts", "wide")),
        P(("parts", "wide"), AXIS),
        P(),
        P(),
        P(),
        P(),
        P(),
    )
    out_specs = P(("parts", "wide"), AXIS, None)
    return jax.shard_map(
        functools.partial(on_device, mesh.shape[AXIS]),
        mesh=mesh,
        in_specs=in_specs,
        out_specs=out_specs,
        check_vma=False,
    )
```
